128 devices in a mesh: row: 16 (over x, y_lo, core), col: 8 (over y_hi, z).
Axes of the slice: x: 4, y: 4 (y_hi: 2, y_lo: 2; y = y_hi * 2 + y_lo), z: 4, core: 2. Of those that a mesh axis runs over, the one named last changes fastest.
Arguments:
- weight: bfloat16 [6144, 6144], P('row', 'col'), may hold values from -6 to 6
- right_op: bfloat16 [8192, 6144], P('row', 'col'), may hold values from -0.078125 to 0.078125
- left_op: bfloat16 [8192, 6144], P('row', 'col'), may hold values from -0.078125 to 0.078125
Outputs:
- grown: bfloat16 [8192, 8192], P(('row', 'col'))
The draws below stay inside these ranges and needn't reach their ends.
All inputs are finite; a program needn't handle non-finite values.
Results may differ from the reference program's by a relative error of at most 0.018.
Values may be sent and summed in bfloat16 or wider, within the bound.
No kernel may reach another device: no remote copies, remote signals or barrier semaphores. Data moves between devices by JAX's collectives and lax.ppermute only.
A program may use at most 64 MiB of HBM per device.

```python
import jax
import jax.numpy as jnp
from jax import lax

DS = 6144
DL = 8192
N_COL = 8


def steps_of(stream_key, dims, shards, low, top_value):
    loudness, own = 1.0, jax.random.fold_in(stream_key, 6)
    for axis_at, shards_of in shards:
        steps = jnp.exp(jax.random.uniform(jax.random.fold_in(own, axis_at), (shards_of,), jnp.float32, low / len(shards), top_value / len(shards)))
        loudness = loudness * jnp.repeat(steps, dims[axis_at] // shards_of).reshape([-1 if axis == axis_at else 1 for axis in range(len(dims))])
    return loudness


def gaussian(own_key, shape, scale, limit, split=(), kind=jnp.bfloat16):
    loudness = steps_of(own_key, shape, split, -0.22, 0.18) if split else 1.0
    entries = jax.random.normal(own_key, shape, jnp.float32) * scale * loudness
    return jnp.minimum(jnp.maximum(entries, -limit), limit).astype(kind)


def setup_inputs(seed: int = 0) -> dict:
    streams_of = jax.random.split(jax.random.key(seed), 4)
    return {
        "weight": gaussian(streams_of[0], (DS, DS), 1.0, 6.0, ((0, 16), (1, 8))),
        "right_op": gaussian(streams_of[1], (DL, DS), DS ** -0.5, 0.078125, ((0, 16), (1, 8))),
        "left_op": gaussian(streams_of[2], (DL, DS), DS ** -0.5, 0.078125, ((0, 16), (1, 8))),
    }


def reference(weight, right_op, left_op):
    block_width = DS // N_COL
    middle = jnp.zeros((DS, DL), jnp.float32)
    for index in range(N_COL):
        first = index * block_width
        term = jnp.dot(weight[:, first:first + block_width], right_op[:, first:first + block_width].T, preferred_element_type=jnp.float32).astype(jnp.bfloat16)
        middle = middle + lax.optimization_barrier(term).astype(jnp.float32)
    middle = middle.astype(jnp.bfloat16)
    grown = jnp.zeros((DL, DL), jnp.float32)
    for index in range(N_COL):
        first = index * block_width
        part = jnp.dot(left_op[:, first:first + block_width], middle[first:first + block_width, :], preferred_element_type=jnp.float32).astype(jnp.bfloat16)
        grown = grown + lax.optimization_barrier(part).astype(jnp.float32)
    return grown.astype(jnp.bfloat16)
```

```python
import jax
import jax.numpy as jnp
from jax import lax
from jax.sharding import PartitionSpec as P

AXES = ("row", "col")
F32, BF16 = jnp.float32, jnp.bfloat16


def pairs(move):
    out = []
    for dev in range(128):
        r, c = dev // 8, dev % 8
        x, yl, k, yh, z = r // 4, (r // 2) % 2, r % 2, c // 4, c % 4
        x, yl, k2, yh, z = move(x, yl, k, yh, z)
        out.append((dev, ((x % 4) * 4 + yl * 2 + k2) * 8 + yh * 4 + z % 4))
    return out


XA = pairs(lambda x, yl, k, yh, z: (x + 1 - 2 * k, yl, k, yh, z))
XB = pairs(lambda x, yl, k, yh, z: (x - 1 + 2 * k, yl, k, yh, z))
YL = pairs(lambda x, yl, k, yh, z: (x, 1 - yl, k, yh, z))
CORE = pairs(lambda x, yl, k, yh, z: (x, yl, 1 - k, yh, z))
YH = pairs(lambda x, yl, k, yh, z: (x, yl, k, 1 - yh, z))
ZA = pairs(lambda x, yl, k, yh, z: (x, yl, k, yh, z + 1 - 2 * k))
ZB = pairs(lambda x, yl, k, yh, z: (x, yl, k, yh, z - 1 + 2 * k))


def send(value, move):
    return lax.ppermute(value, AXES, move)


def pick(stack, index):
    return lax.dynamic_index_in_dim(stack, index, 0, keepdims=False)


def shards(weight, right_op, left_op):
    row, col = lax.axis_index("row"), lax.axis_index("col")
    x, yl, k, yh, z = row // 4, (row // 2) % 2, row % 2, col // 4, col % 4
    sign = 1 - 2 * k
    wr, wc = weight.shape
    rr, half = right_op.shape[0], right_op.shape[0] // 2
    piece = left_op.shape[0] // 8

    w0 = weight
    wa, wb, wy = send(w0, XA), send(w0, XB), send(w0, YL)
    wya, wyb = send(wy, XA), send(wy, XB)
    w_c, wyc = send(wa, XA), send(wya, XA)

    mine = lax.dynamic_slice_in_dim(left_op, k * wr, wr, 1)
    other = lax.dynamic_slice_in_dim(left_op, (1 - k) * wr, wr, 1)

    def by_owner(v):
        return v.reshape(2, 4, piece, wr).transpose(1, 0, 2, 3).reshape(8 * piece, wr)

    l0 = jnp.concatenate([by_owner(mine), send(by_owner(other), CORE)], 0)
    la, lb, ly = send(l0, ZA), send(l0, ZB), send(l0, YH)
    lya, lyb = send(ly, ZA), send(ly, ZB)
    lc, lyc = send(la, ZA), send(lya, ZA)

    keep = lax.dynamic_slice_in_dim(right_op, yh * half, half, 0)
    give = lax.dynamic_slice_in_dim(right_op, (1 - yh) * half, half, 0)
    r1 = jnp.concatenate([keep, send(give, YH)], 1)
    r2 = jnp.concatenate([r1, send(r1, YL)], 0)
    ra, rb = send(r2, XA), send(r2, XB)
    rc = send(ra, XA)
    rg = jnp.concatenate([r2, ra, rb, rc], 0)

    wg = jnp.stack([w0, wa, w_c, wb, wy, wya, wyc, wyb])

    def term(lv, dyh, dz):
        c2 = (yh ^ dyh) * 4 + (z + dz) % 4
        x2, yl2 = c2 // 2, c2 % 2
        slot = (yl ^ yl2) * 4 + (sign * (x - x2)) % 4
        return jnp.dot(lv, pick(wg, slot), preferred_element_type=F32)

    total = term(l0, 0, 0)
    for lv, dyh, dz in ((la, 0, -sign), (lb, 0, sign), (ly, 1, 0), (lc, 0, 2), (lya, 1, -sign), (lyb, 1, sign), (lyc, 1, 2)):
        total = total + term(lv, dyh, dz)
    rows = 8 * piece
    t1 = (total[:rows] + send(total[rows:].astype(BF16), CORE).astype(F32)).astype(BF16)
    t2 = jnp.concatenate([t1, send(t1, YH)], 1)
    t = jnp.stack([t2, send(t2, CORE)]).reshape(2, 4, 2 * piece, 2 * wc)

    def part(dz):
        td = lax.dynamic_index_in_dim(t, (z + dz) % 4, 1, keepdims=False).reshape(4 * piece, 2 * wc)
        return jnp.einsum("ib,jb->ij", td, rg, preferred_element_type=F32)

    s1 = send(part(2).astype(BF16), ZA)
    s2 = send((part(sign) + s1.astype(F32)).astype(BF16), ZA)
    s3 = send(part(-sign).astype(BF16), ZB)
    own = (part(0) + s2.astype(F32) + s3.astype(F32)).astype(BF16)
    own = own.reshape(2, 2, piece, 4 * rr)
    o_keep = lax.dynamic_index_in_dim(own, yh, 1, keepdims=False)
    o_give = lax.dynamic_index_in_dim(own, 1 - yh, 1, keepdims=False)
    both = jnp.stack([o_keep, send(o_give, YH)])
    fin = jnp.stack([both[:, 0], send(both[:, 1], CORE)])
    blocks = fin.reshape(2, 2, piece, 8, half).transpose(0, 1, 3, 2, 4).reshape(32, piece, half)
    n = jnp.arange(32)
    x2, yl2, k2, h2 = n // 8, (n // 4) % 2, (n // 2) % 2, n % 2
    d = ((1 - 2 * k2) * (x - x2)) % 4
    slot = jnp.where(d >= 2, 5 - d, d)
    index = (((k2 ^ k) * 2 + (h2 ^ yh)) * 4 + slot) * 2 + (yl2 ^ yl)
    return blocks[index].transpose(1, 0, 2).reshape(piece, 32 * half)


def solution(mesh):
    spec = P("row", "col")
    return jax.shard_map(shards, mesh=mesh, in_specs=(spec, spec, spec), out_specs=P(AXES, None), check_vma=False)
```

```python
import jax
import jax.numpy as jnp
from jax import lax
from jax.sharding import PartitionSpec as P

AXES = ("row", "col")
F32, BF16 = jnp.float32, jnp.bfloat16


def pairs(move):
    out = []
    for dev in range(128):
        r, c = dev // 8, dev % 8
        x, yl, k, yh, z = r // 4, (r // 2) % 2, r % 2, c // 4, c % 4
        x, yl, k2, yh, z = move(x, yl, k, yh, z)
        out.append((dev, ((x % 4) * 4 + yl * 2 + k2) * 8 + yh * 4 + z % 4))
    return out


XA = pairs(lambda x, yl, k, yh, z: (x + 1 - 2 * k, yl, k, yh, z))
XB = pairs(lambda x, yl, k, yh, z: (x - 1 + 2 * k, yl, k, yh, z))
YL = pairs(lambda x, yl, k, yh, z: (x, 1 - yl, k, yh, z))
CORE = pairs(lambda x, yl, k, yh, z: (x, yl, 1 - k, yh, z))
YH = pairs(lambda x, yl, k, yh, z: (x, yl, k, 1 - yh, z))
ZA = pairs(lambda x, yl, k, yh, z: (x, yl, k, yh, z + 1 - 2 * k))
ZB = pairs(lambda x, yl, k, yh, z: (x, yl, k, yh, z - 1 + 2 * k))


def send(value, move):
    return lax.ppermute(value, AXES, move)


def pick(stack, index, axis=0):
    return lax.dynamic_index_in_dim(stack, index, axis, keepdims=False)


def inner(weight, right_op, left_op):
    row, col = lax.axis_index("row"), lax.axis_index("col")
    x, yl, k, yh, z = row // 4, (row // 2) % 2, row % 2, col // 4, col % 4
    sign = 1 - 2 * k
    wr, wc = weight.shape
    rr, half = right_op.shape[0], right_op.shape[0] // 2
    piece = left_op.shape[0] // 8

    w0 = weight
    wa, wb, wy = send(w0, XA), send(w0, XB), send(w0, YL)
    wya, wyb = send(wy, XA), send(wy, XB)
    wcc, wyc = send(wa, XA), send(wya, XA)

    mine = lax.dynamic_slice_in_dim(left_op, k * wr, wr, 1)
    other = lax.dynamic_slice_in_dim(left_op, (1 - k) * wr, wr, 1)
    l0 = jnp.concatenate([mine, send(other, CORE)], 0)
    la, lb, ly = send(l0, ZA), send(l0, ZB), send(l0, YH)
    lya, lyb = send(ly, ZA), send(ly, ZB)
    lc, lyc = send(la, ZA), send(lya, ZA)

    keep = lax.dynamic_slice_in_dim(right_op, yh * half, half, 0)
    give = lax.dynamic_slice_in_dim(right_op, (1 - yh) * half, half, 0)
    got = send(give, YH)
    r0 = jnp.concatenate([keep, got], 1)
    ra, rb, ry = send(r0, XA), send(r0, XB), send(r0, YL)
    rya, ryb = send(ry, XA), send(ry, XB)
    rc, ryc = send(ra, XA), send(rya, XA)
    rga = jnp.concatenate([r0, ry, ra, rb], 0)
    rgb = jnp.concatenate([rc, rya, ryb, ryc], 0)
    rg = (rga, rgb)

    wg = jnp.stack([w0, wa, wcc, wb, wy, wya, wyc, wyb])

    def term(lv, dyh, dz):
        c2 = (yh ^ dyh) * 4 + (z + dz) % 4
        x2, yl2 = c2 // 2, c2 % 2
        slot = (yl ^ yl2) * 4 + (sign * (x - x2)) % 4
        return jnp.dot(lv, pick(wg, slot), preferred_element_type=F32)

    total = term(l0, 0, 0)
    for lv, dyh, dz in ((la, 0, -sign), (lb, 0, sign), (ly, 1, 0), (lc, 0, 2), (lya, 1, -sign), (lyb, 1, sign), (lyc, 1, 2)):
        total = total + term(lv, dyh, dz)
    total = total.reshape(2, 2, 4, piece, wc)

    def whole(dzs):
        p = jnp.stack([pick(total, (z + dz) % 4, 2) for dz in dzs], 1)
        p = p.reshape(2, len(dzs) * 2 * piece, wc)
        t1 = (p[0] + send(p[1].astype(BF16), CORE).astype(F32)).astype(BF16)
        t2 = jnp.concatenate([t1, send(t1, YH)], 1)
        return jnp.stack([t2, send(t2, CORE)]).reshape(2, len(dzs), 2 * piece, 2 * wc)

    tf = whole((2,))
    tn = whole((1, -1, 0))

    def part(td, c):
        return jnp.einsum("ib,jb->ij", td.reshape(4 * piece, 2 * wc), rg[c], preferred_element_type=F32)

    keeps, gives = [], []
    for c, n in enumerate("ab"):
        s1 = send(part(tf[:, 0], c).astype(BF16), ZA)
        s2 = send((part(pick(tn, k, 1), c) + s1.astype(F32)).astype(BF16), ZA)
        s3 = send(part(pick(tn, 1 - k, 1), c).astype(BF16), ZB)
        own = (part(tn[:, 2], c) + s2.astype(F32) + s3.astype(F32)).astype(BF16)
        own = own.reshape(2, 2, piece, 2 * rr)
        keeps.append(pick(own, yh, 1))
        gives.append(send(pick(own, 1 - yh, 1), YH))
    both = jnp.stack(keeps + gives)
    fin = jnp.stack([both[:, 0], send(both[:, 1], CORE)])
    blocks = fin.reshape(2, 4, piece, 4, half).transpose(0, 1, 3, 2, 4).reshape(32, piece, half)
    n = jnp.arange(32)
    x2, yl2, k2, h2 = n // 8, (n // 4) % 2, (n // 2) % 2, n % 2
    d = ((1 - 2 * k2) * (x - x2)) % 4
    slot = jnp.array([[0, 2, 4, 3], [1, 5, 7, 6]])[yl2 ^ yl, d]
    index = ((k2 ^ k) * 2 + (h2 ^ yh)) * 8 + slot
    return blocks[index].transpose(1, 0, 2).reshape(piece, 32 * half)


def solution(mesh):
    spec = P("row", "col")
    return jax.shard_map(inner, mesh=mesh, in_specs=(spec, spec, spec), out_specs=P(AXES, None), check_vma=False)
```

```python
import functools

import jax
import jax.numpy as jnp
import numpy as np
from jax import lax
from jax.experimental import pallas as pl
from jax.experimental.pallas import tpu as pltpu
from jax.sharding import PartitionSpec as P

AXES = ("row", "col")
F32, BF16 = jnp.float32, jnp.bfloat16


def pairs(move):
    out = []
    for dev in range(128):
        r, c = dev // 8, dev % 8
        x, yl, k, yh, z = r // 4, (r // 2) % 2, r % 2, c // 4, c % 4
        x, yl, k2, yh, z = move(x, yl, k, yh, z)
        out.append((dev, ((x % 4) * 4 + yl * 2 + k2) * 8 + yh * 4 + z % 4))
    return out


XA = pairs(lambda x, yl, k, yh, z: (x + 1 - 2 * k, yl, k, yh, z))
XB = pairs(lambda x, yl, k, yh, z: (x - 1 + 2 * k, yl, k, yh, z))
YL = pairs(lambda x, yl, k, yh, z: (x, 1 - yl, k, yh, z))
CORE = pairs(lambda x, yl, k, yh, z: (x, yl, 1 - k, yh, z))
YH = pairs(lambda x, yl, k, yh, z: (x, yl, k, 1 - yh, z))
ZA = pairs(lambda x, yl, k, yh, z: (x, yl, k, yh, z + 1 - 2 * k))
ZB = pairs(lambda x, yl, k, yh, z: (x, yl, k, yh, z - 1 + 2 * k))


def send(value, move):
    return lax.ppermute(value, AXES, move)


def pick(stack, index, axis=0):
    return lax.dynamic_index_in_dim(stack, index, axis, keepdims=False)


VMEM, SMEM = pl.BlockSpec(memory_space=pltpu.VMEM), pl.BlockSpec(memory_space=pltpu.SMEM)


def early_terms(table, *refs):
    w_refs, l_refs, (total, *rest, stack) = refs[:8], refs[8:13], refs[13:]
    for q, w in enumerate(w_refs):
        stack[table[q]] = w[...]
    for q, w in enumerate(rest):
        w[...] = stack[5 + q]
    _, rows, depth = l_refs[0].shape[1:]
    columns = total.shape[3]

    def group(g, carry):
        lv = jnp.concatenate([v[:, g].reshape(4 * rows, depth) for v in l_refs], 1)
        acc = jnp.dot(lv, stack[:5].reshape(5 * depth, columns), preferred_element_type=F32)
        total[:, g] = acc.reshape(4, rows, columns)
        return carry

    lax.fori_loop(0, 4, group, 0)


def products(table, *refs, pieces, groups, added):
    t_refs, r_refs = refs[: 2 * len(groups)], refs[2 * len(groups) :][:pieces]
    dests = sum(groups)
    outs, lhs = refs[-1 - dests : -1], refs[-1]
    first = refs[-2 - dests] if added else None
    rows, width = t_refs[0].shape[0] // groups[0], r_refs[0].shape[0]
    j = 0
    for g, count in enumerate(groups):
        near, far = t_refs[2 * g], t_refs[2 * g + 1]
        for _ in range(count):
            at = pl.ds(pl.multiple_of(table[j] * rows, rows), rows)
            lhs[2 * j * rows : (2 * j + 1) * rows] = near[at, :]
            lhs[(2 * j + 1) * rows : (2 * j + 2) * rows] = far[at, :]
            j += 1
    for i, r in enumerate(r_refs):
        acc = lax.dot_general(lhs[...], r[...], (((1,), (1,)), ((), ())), preferred_element_type=F32)
        for j, out in enumerate(outs):
            block = acc[2 * j * rows : (2 * j + 2) * rows]
            if j == 0 and added:
                block = block + first[:, i * width : (i + 1) * width].astype(F32)
            out[:, i * width : (i + 1) * width] = block.astype(BF16)


def place(where, *refs):
    parts, other, out = refs[:4], refs[4], refs[5]
    width, split = out.shape[1] // 32, parts[0].shape[2]
    for n in range(32):
        core, h, slot = n // 16, (n // 8) % 2, n % 8
        first = slot * width
        if core:
            block = other[h, :, first : first + width]
        elif first < split:
            block = parts[2 * h][0, :, first : first + width]
        else:
            block = parts[2 * h + 1][0, :, first - split : first - split + width]
        out[:, pl.ds(pl.multiple_of(where[n] * width, width), width)] = block


def inner(weight, right_op, left_op):
    row, col = lax.axis_index("row"), lax.axis_index("col")
    x, yl, k, yh, z = row // 4, (row // 2) % 2, row % 2, col // 4, col % 4
    sign = 1 - 2 * k
    wr, wc = weight.shape
    half = right_op.shape[0] // 2
    piece = left_op.shape[0] // 8
    rows = 8 * piece

    w0 = weight
    wa, wb, wy = send(w0, XA), send(w0, XB), send(w0, YL)
    wya, wyb = send(wy, XA), send(wy, XB)
    wcc, wyc = send(wa, XA), send(wya, XA)

    mine = lax.dynamic_slice_in_dim(left_op, k * wr, wr, 1)
    other = lax.dynamic_slice_in_dim(left_op, (1 - k) * wr, wr, 1)
    l0 = jnp.concatenate([mine, send(other, CORE)], 0)
    la, lb, ly = send(l0, ZA), send(l0, ZB), send(l0, YH)
    lya, lyb = send(ly, ZA), send(ly, ZB)
    lc, lyc = send(la, ZA), send(lya, ZA)

    keep = lax.dynamic_slice_in_dim(right_op, yh * half, half, 0)
    give = lax.dynamic_slice_in_dim(right_op, (1 - yh) * half, half, 0)
    got = send(give, YH)
    r0 = jnp.concatenate([keep, got], 1)
    ra, rb, ry = send(r0, XA), send(r0, XB), send(r0, YL)
    rya, ryb = send(ry, XA), send(ry, XB)
    ryc = send(rya, XA)

    def order(dx, dyl):
        c2 = (x + dx) % 4 * 2 + (yl ^ dyl)
        step = sign * (z - c2 % 4) % 4
        near = jnp.where(step < 2, step, 5 - step)
        far = 4 + jnp.where(step < 2, step, 5 - step)
        return jnp.where(c2 // 4 == yh, near, far)

    steps = (0, -sign, 2, sign)
    table = jnp.stack([order(dx, dyl) for dyl in (0, 1) for dx in steps]).astype(jnp.int32)
    ls = [v.reshape(4, 4, piece, wr) for v in (l0, la, lb, lc, ly)]
    flops = 2 * rows * 2 * wr * wc
    total, *rest = pl.pallas_call(
        early_terms,
        out_shape=[jax.ShapeDtypeStruct((4, 4, piece, wc), F32)] + [jax.ShapeDtypeStruct((wr, wc), BF16)] * 3,
        in_specs=[SMEM] + [VMEM] * 13,
        out_specs=[VMEM] * 4,
        scratch_shapes=[pltpu.VMEM((8, wr, wc), BF16)],
        cost_estimate=pl.CostEstimate(flops=5 * flops, bytes_accessed=13_000_000, transcendentals=0),
        compiler_params=pltpu.CompilerParams(vmem_limit_bytes=32 << 20),
    )(table, w0, wa, wcc, wb, wy, wya, wyc, wyb, *ls)
    total = total.reshape(2 * rows, wc)
    for lv, w in ((lya, rest[0]), (lyb, rest[1])):
        total = total + jnp.dot(lv, w, preferred_element_type=F32)
    total = total + jnp.dot(lyc, rest[2], preferred_element_type=F32)
    total = total.reshape(2, 2, 4, piece, wc)

    rc = send(ra, XA)

    def whole(dzs):
        p = jnp.stack([pick(total, (z + dz) % 4, 2) for dz in dzs], 1).reshape(2, -1, wc)
        t1 = (p[0] + send(p[1].astype(BF16), CORE).astype(F32)).astype(BF16)
        t2 = jnp.concatenate([t1, send(t1, YH)], 1)
        return t2, send(t2, CORE)

    tf = whole((2,))
    tn = whole((1, -1))
    tz = whole((0,))

    def part(table, ts, rs, *first):
        groups = tuple(t[0].shape[0] // (2 * piece) for t in ts)
        dests, depth, columns = sum(groups), 2 * wc, len(rs) * half
        return pl.pallas_call(
            functools.partial(products, pieces=len(rs), groups=groups, added=len(first)),
            out_shape=[jax.ShapeDtypeStruct((4 * piece, columns), BF16)] * dests,
            in_specs=[SMEM] + [VMEM] * (2 * len(ts) + len(rs) + len(first)),
            out_specs=[VMEM] * dests,
            scratch_shapes=[pltpu.VMEM((4 * piece * dests, depth), BF16)],
            cost_estimate=pl.CostEstimate(
                flops=8 * piece * dests * depth * columns, bytes_accessed=6_000_000, transcendentals=0
            ),
            compiler_params=pltpu.CompilerParams(vmem_limit_bytes=24 << 20),
        )(jnp.stack(table).astype(jnp.int32), *[v for t in ts for v in t], *rs, *first)

    def finish(own, *received):
        def half_of(h):
            vs = [pick(v.reshape(2, 2, piece, -1), h, 1).astype(F32) for v in (own, *received)]
            return (vs[0] + vs[1] + vs[2]).astype(BF16)

        gives.append(send(half_of(1 - yh), YH))
        keeps.append(half_of(yh))

    keeps, gives, zero = [], [], k * 0
    ra_s, rb_s = (r0, ry, ra, rb), (rc, rya, ryb, ryc)
    s1 = send(part([zero], [tf], ra_s)[0], ZA)
    ahead, back = part([k, 1 - k], [tn], ra_s, s1)
    s2, s3 = send(ahead, ZA), send(back, ZB)
    own = part([zero], [tz], ra_s)[0]
    finish(own, s2, s3)
    far, ahead, back, own = part([zero, k, 1 - k, zero], [tf, tn, tz], rb_s)
    s1 = send(far, ZA)
    s2, s3 = send((ahead.astype(F32) + s1.astype(F32)).astype(BF16), ZA), send(back, ZB)
    finish(own, s2, s3)
    parts = [keeps[0], keeps[1], gives[0], gives[1]]
    other = jnp.stack([jnp.concatenate([keeps[0][1], keeps[1][1]], 1), jnp.concatenate([gives[0][1], gives[1][1]], 1)])
    n = np.arange(32)
    k2, h2, slots = k ^ (n // 16), yh ^ ((n // 8) % 2), n % 8
    d = np.array([0, 0, 1, 3, 2, 1, 3, 2])[slots]
    yl2 = yl ^ np.array([0, 1, 0, 0, 0, 1, 1, 1])[slots]
    where = (((x - (1 - 2 * k2) * d) % 4 * 2 + yl2) * 2 + k2) * 2 + h2
    return pl.pallas_call(
        place,
        out_shape=jax.ShapeDtypeStruct((piece, 32 * half), BF16),
        in_specs=[SMEM] + [VMEM] * 5,
        out_specs=VMEM,
        cost_estimate=pl.CostEstimate(flops=0, bytes_accessed=2_000_000, transcendentals=0),
        compiler_params=pltpu.CompilerParams(vmem_limit_bytes=8 << 20),
    )(where.astype(jnp.int32), *parts, send(other, CORE))


def solution(mesh):
    spec = P("row", "col")
    return jax.shard_map(inner, mesh=mesh, in_specs=(spec, spec, spec), out_specs=P(AXES, None), check_vma=False)
```
